32 devices in a mesh: days: 2 (over x), chan: 16 (over z, y, core).
Axes of the slice: x: 2, y: 2, z: 4, core: 2. Of those that a mesh axis runs over, the one named last changes fastest.
Arguments:
- spectra: bfloat16 [8, 512, 2048], P('days', None, 'chan'), may hold values from -6 to 6
- sources: int32 [2], replicated, may hold values from 0 to 2047
- offsets: int32 [2048], P('chan'), may hold values from 0 to 4095
Outputs:
- slant: float32 [128, 2, 2, 256], P('chan')
The draws below stay inside these ranges and needn't reach their ends.
All inputs are finite; a program needn't handle non-finite values.
Results may differ from the reference program's by a relative error of at most 0.0055.
Values may be sent and summed in bfloat16 or wider, within the bound.
A program may use at most 64 MiB of HBM per device.

```python
import math
import jax
import jax.numpy as jnp
from jax import lax

BINS = 256
LAGS = 512
NSLOW = 128
NSRC = 2
CHANNELS = 2048
WINDOWS = 8


def touch_ends(array, key, low, top_value):
    shape = array.shape
    place = [jax.random.randint(jax.random.fold_in(key, axis), (), 0, shape[axis]) for axis in range(len(shape))]
    array = array.at[tuple(place)].set(low)
    longest = shape.index(max(shape))
    place[longest] = (place[longest] + 1) % shape[longest]
    return array.at[tuple(place)].set(top_value)


def block_levels(own_key, dims, shards, smallest, largest):
    level, own = 1.0, jax.random.fold_in(own_key, 6)
    for position, shards_of in shards:
        steps = jnp.exp(jax.random.uniform(jax.random.fold_in(own, position), (shards_of,), jnp.float32, smallest / len(shards), largest / len(shards)))
        level = level * jnp.repeat(steps, dims[position] // shards_of).reshape([-1 if axis == position else 1 for axis in range(len(dims))])
    return level


def noise(own_key, shape, spread, reach, cuts=(), kind=jnp.bfloat16):
    loudness = block_levels(own_key, shape, cuts, -0.22, 0.18) if cuts else 1.0
    result = jax.random.normal(own_key, shape, jnp.float32) * spread * loudness
    return jnp.minimum(jnp.maximum(result, -reach), reach).astype(kind)


def setup_inputs(seed: int = 0) -> dict:
    key_of = jax.random.split(jax.random.key(seed), 4)
    spectra = noise(key_of[0], (WINDOWS, 2 * BINS, CHANNELS), 1.0, 6.0, ((0, 2), (2, 16)))
    sources = jax.random.randint(key_of[1], (NSRC,), 0, CHANNELS).astype(jnp.int32)
    offsets = touch_ends(jax.random.randint(key_of[2], (CHANNELS,), 0, 4096), jax.random.fold_in(key_of[2], 1), 0, 4095).astype(jnp.int32)
    return {"spectra": spectra, "sources": sources, "offsets": offsets}


def angles(left_index, right_index, period):
    return (left_index * right_index % period).astype(jnp.float32) * (2.0 * math.pi / period)

def inverse_table(bins):
    lag_total = 2 * bins
    theta = angles(jnp.arange(lag_total, dtype=jnp.int32)[:, None], jnp.arange(bins, dtype=jnp.int32)[None, :], lag_total)
    cosine = jnp.cos(theta)
    sine = jnp.sin(theta)
    upper = jnp.concatenate([cosine, -sine], 1)
    lower = jnp.concatenate([sine, cosine], 1)
    return (jnp.concatenate([upper, lower], 0) / math.sqrt(bins)).astype(jnp.bfloat16)

def forward_table(bins, lag_first, lag_count):
    lag_total = 2 * bins
    theta = angles(jnp.arange(bins, dtype=jnp.int32)[:, None], lag_first + jnp.arange(lag_count, dtype=jnp.int32)[None, :], lag_total)
    return jnp.concatenate([jnp.cos(theta), -jnp.sin(theta)], 0) / math.sqrt(lag_total)

def slant_block(spec_re, spec_im, slowness, offsets, bins):
    freq = jnp.arange(bins, dtype=jnp.int32)
    phase = freq[None, :, None] * slowness[:, None, None] % 4096 * offsets[None, None, :] % 4096
    theta = phase.astype(jnp.float32) * (2.0 * math.pi / 4096)
    cosine = jnp.cos(theta)
    sine = jnp.sin(theta)
    highest = lax.Precision.HIGHEST
    real_part = jnp.einsum('sfc,kfc->ksf', spec_re, cosine, precision=highest) - jnp.einsum('sfc,kfc->ksf', spec_im, sine, precision=highest)
    imag_part = jnp.einsum('sfc,kfc->ksf', spec_re, sine, precision=highest) + jnp.einsum('sfc,kfc->ksf', spec_im, cosine, precision=highest)
    return jnp.stack([real_part, imag_part], 2)

def reference(spectra, sources, offsets):
    inverse = inverse_table(BINS).astype(jnp.float32)
    highest = lax.Precision.HIGHEST

    def one_window(totals, window):
        source_part = window[:, sources].T.astype(jnp.float32)
        channel_part = window.astype(jnp.float32)
        real_s = source_part[:, :BINS, None]
        imag_s = source_part[:, BINS:, None]
        real_x = channel_part[None, :BINS]
        imag_x = channel_part[None, BINS:]
        product = jnp.concatenate([real_s * real_x + imag_s * imag_x, real_s * imag_x - imag_s * real_x], 1)
        rounded = lax.optimization_barrier(product.astype(jnp.bfloat16)).astype(jnp.float32)
        analytic = jnp.einsum('lk,skc->slc', inverse, rounded, precision=highest)
        correlation = analytic[:, :LAGS]
        hilbert = analytic[:, LAGS:]
        magnitude = jnp.maximum(jnp.sqrt(correlation * correlation + hilbert * hilbert), 0.5)
        return ((totals[0] + correlation, totals[1] + correlation / magnitude, totals[2] + hilbert / magnitude), None)
    empty = jnp.zeros((NSRC, LAGS, CHANNELS), jnp.float32)
    (linear, phase_re, phase_im), _ = lax.scan(one_window, (empty, empty, empty), spectra)
    weighted = linear / WINDOWS * ((phase_re * phase_re + phase_im * phase_im) / (WINDOWS * WINDOWS))
    forward = forward_table(BINS, 0, LAGS)
    spectrum = jnp.einsum('kt,stc->skc', forward, weighted, precision=highest)
    spec_re = spectrum[:, :BINS]
    spec_im = spectrum[:, BINS:]
    scaling = WINDOWS ** 1.5 / math.sqrt(CHANNELS)
    group_size = math.gcd(NSLOW, 8)
    groups = jnp.arange(NSLOW, dtype=jnp.int32).reshape(NSLOW // group_size, group_size)

    def one_group(slowness):
        return slant_block(spec_re, spec_im, slowness, offsets, BINS)
    pieces = lax.map(one_group, groups)
    return pieces.reshape(NSLOW, NSRC, 2, BINS) * scaling
```

```python
import functools
import math

import jax
import jax.numpy as jnp
import numpy as np
from jax import lax
from jax.experimental import pallas as pl
from jax.experimental.pallas import tpu as pltpu
from jax.sharding import PartitionSpec as P

NSLOW = 128
NSRC = 2
PERIOD = 4096
TILE = 8
LANES = 128
GROUP = 2


def tables(bins):
    lag_total = 2 * bins
    lag = np.arange(lag_total)[:, None]
    freq = np.arange(bins)[None, :]
    theta = (lag * freq % lag_total) * (2.0 * math.pi / lag_total)
    cosine, sine = np.cos(theta), np.sin(theta)
    inverse = np.concatenate(
        [np.concatenate([cosine, -sine], 1), np.concatenate([sine, cosine], 1)], 0
    ) / math.sqrt(bins)
    forward = np.concatenate([cosine, -sine], 1) / math.sqrt(lag_total)
    return (
        inverse.astype(np.float32).astype(jnp.bfloat16),
        forward.astype(np.float32).astype(jnp.bfloat16),
    )


def cos_sin(steps):
    quarter = PERIOD // 4
    place = steps & (PERIOD - 1)
    quadrant = (place + quarter // 2) // quarter
    x = (place - quadrant * quarter).astype(jnp.float32) * (2.0 * math.pi / PERIOD)
    y = x * x
    sine = x * (1.0 + y * (-1.0 / 6 + y * (1.0 / 120 - y * (1.0 / 5040))))
    cosine = 1.0 + y * (-0.5 + y * (1.0 / 24 + y * (-1.0 / 720 + y * (1.0 / 40320))))
    odd = (quadrant & 1) == 1
    first = jnp.where(odd, sine, cosine)
    second = jnp.where(odd, cosine, sine)
    first = jnp.where(((quadrant + 1) & 2) == 2, -first, first)
    second = jnp.where((quadrant & 2) == 2, -second, second)
    return first, second


def correlate(x_ref, s_ref, inverse_ref, forward_ref, analytic, weighted, spectrum, windows):
    count, depth, width = x_ref.shape
    bins, half = depth // 2, width // 2
    lags = depth
    wide = NSRC * width
    rows = lax.broadcasted_iota(jnp.int32, (s_ref.shape[1], wide), 0)
    lane = lax.broadcasted_iota(jnp.int32, (s_ref.shape[1], wide), 1)
    wanted = lane // width * 2 + lane % width // half
    for w in range(count):
        pick = (rows == w * (2 * NSRC) + wanted).astype(jnp.float32).astype(jnp.bfloat16)
        source = jnp.dot(s_ref[...], pick, preferred_element_type=jnp.float32)
        channel = x_ref[w].astype(jnp.float32)
        channel = jnp.concatenate([channel] * NSRC, 1)
        real_s, imag_s = source[:bins], source[bins:]
        real_x, imag_x = channel[:bins], channel[bins:]
        product = jnp.concatenate(
            [real_s * real_x + imag_s * imag_x, real_s * imag_x - imag_s * real_x], 0
        ).astype(jnp.bfloat16)
        analytic[w] = jnp.dot(inverse_ref[...], product, preferred_element_type=jnp.float32)

    block = 16

    def stack(step, carry):
        start = pl.multiple_of(step * block, block)
        linear = phase_re = phase_im = 0.0
        for w in range(count):
            corr = analytic[w, pl.ds(start, block)]
            hilb = analytic[w, pl.ds(lags + start, block)]
            over = jnp.minimum(lax.rsqrt(corr * corr + hilb * hilb), 2.0)
            linear = linear + corr
            phase_re = phase_re + corr * over
            phase_im = phase_im + hilb * over

        def fold(value):
            parts = []
            for s in range(NSRC):
                part = value[:, s * width : (s + 1) * width]
                parts.append(part + pltpu.roll(part, half, 1))
            side = lax.broadcasted_iota(jnp.int32, (block, width), 1) < half
            return jnp.where(side, parts[0], parts[1])

        linear, phase_re, phase_im = fold(linear), fold(phase_re), fold(phase_im)
        result = linear * (phase_re * phase_re + phase_im * phase_im) * (1.0 / windows**3)
        weighted[pl.ds(start, block)] = result.astype(jnp.bfloat16)
        return carry

    lax.fori_loop(0, lags // block, stack, 0)
    result = lax.dot_general(
        weighted[...], forward_ref[...], (((0,), (0,)), ((), ())), preferred_element_type=jnp.float32
    )
    for part in range(depth // LANES):
        spectrum[part] = result[:, part * LANES : (part + 1) * LANES]


def slant(offset_ref, spectrum, base, out_ref, half, bins, scaling):
    out_ref[...] = jnp.zeros_like(out_ref)
    steps = NSLOW // TILE
    low = lax.broadcasted_iota(jnp.int32, (TILE, LANES), 0)
    for part in range(bins // LANES):
        freq = lax.broadcasted_iota(jnp.int32, (TILE, LANES), 1) + part * LANES
        product = low * freq
        lanes = pl.ds(part * LANES, LANES)
        part_im = bins // LANES + part

        def group(number, carry):
            now, before, twice = [], [], []
            for member in range(GROUP):
                channel = number * GROUP + member
                offset = offset_ref[base + channel]
                jump_cos, jump_sin = cos_sin(freq * (offset * TILE))
                cosine, sine = cos_sin(product * offset)
                back_cos = cosine * jump_cos + sine * jump_sin
                back_sin = sine * jump_cos - cosine * jump_sin
                twice.append(2.0 * jump_cos)
                for s in range(NSRC):
                    row = pl.ds(s * half + channel, 1)
                    real = spectrum[part, row] * scaling
                    imag = spectrum[part_im, row] * scaling
                    now.append([real * cosine - imag * sine, real * sine + imag * cosine])
                    before.append([real * back_cos - imag * back_sin, real * back_sin + imag * back_cos])
            for step in range(steps):
                for s in range(NSRC):
                    for piece in range(2):
                        total = now[s][piece]
                        for member in range(1, GROUP):
                            total = total + now[member * NSRC + s][piece]
                        here = (s, piece, pl.ds(step * TILE, TILE), lanes)
                        out_ref[here] = out_ref[here] + total
                if step + 1 < steps:
                    for member in range(GROUP):
                        for s in range(NSRC):
                            at = member * NSRC + s
                            for piece in range(2):
                                later = twice[member] * now[at][piece] - before[at][piece]
                                before[at][piece] = now[at][piece]
                                now[at][piece] = later
            return carry

        lax.fori_loop(0, half // GROUP, group, 0)


def compute_kernel(windows, scaling, x_ref, s_ref, inverse_ref, forward_ref, offset_ref, out_ref, analytic, weighted, spectrum):
    half, bins = x_ref.shape[2] // 2, x_ref.shape[1] // 2
    correlate(x_ref, s_ref, inverse_ref, forward_ref, analytic, weighted, spectrum, windows)
    slant(offset_ref, spectrum, 0, out_ref, half, bins, scaling)


def shards(spectra, sources, offsets):
    count, depth, width = spectra.shape
    bins, half = depth // 2, width // 2
    day_devices, chan_devices = lax.axis_size("days"), lax.axis_size("chan")
    windows = count * day_devices
    me = lax.axis_index("days")
    swap = [(0, 1), (1, 0)]
    collected = []
    for number in range(NSRC):
        holder = sources[number] // width
        column = sources[number] - holder * width
        single = lax.dynamic_slice_in_dim(spectra, column, 1, 2)[:, :, 0]
        collected.append(jnp.where(lax.axis_index("chan") == holder, single, 0).astype(spectra.dtype))
    own = lax.psum(jnp.stack(collected, 1), "chan")
    other = lax.ppermute(own, "days", swap)
    source = jnp.stack([own, other], 2).transpose(3, 0, 1, 2).reshape(depth, count * NSRC * 2)
    kept = lax.dynamic_slice_in_dim(spectra, me * half, half, 2)
    sent = lax.dynamic_slice_in_dim(spectra, (1 - me) * half, half, 2)
    got = lax.ppermute(sent, "days", swap)
    paired = jnp.concatenate([kept, got], 2)
    inverse, forward = tables(bins)
    mine = lax.dynamic_slice_in_dim(offsets, me * half, half, 0)
    scaling = windows**1.5 / math.sqrt(width * chan_devices)
    vmem = pl.BlockSpec(memory_space=pltpu.VMEM)
    partial = pl.pallas_call(
        functools.partial(compute_kernel, windows, scaling),
        out_shape=jax.ShapeDtypeStruct((NSRC, 2, NSLOW, bins), jnp.float32),
        in_specs=[vmem] * 4 + [pl.BlockSpec(memory_space=pltpu.SMEM)],
        out_specs=vmem,
        scratch_shapes=[
            pltpu.VMEM((count, 2 * depth, NSRC * width), jnp.float32),
            pltpu.VMEM((depth, width), jnp.bfloat16),
            pltpu.VMEM((depth // LANES, NSRC * half, LANES), jnp.float32),
        ],
    )(paired, source, jnp.asarray(inverse), jnp.asarray(forward), mine)
    owned = lax.psum_scatter(partial.transpose(2, 0, 1, 3), "chan", scatter_dimension=0, tiled=True)
    return lax.psum(owned, "days")


def solution(mesh):
    placed = (P("days", None, "chan"), P(), P("chan"))
    return jax.shard_map(
        shards, mesh=mesh, in_specs=placed, out_specs=P("chan", None, None, None), check_vma=False
    )
```

```python
import functools
import math

import jax
import jax.numpy as jnp
import numpy as np
from jax import lax
from jax.experimental import pallas as pl
from jax.experimental.pallas import tpu as pltpu
from jax.sharding import PartitionSpec as P

NSLOW = 128
NSRC = 2
PERIOD = 4096
TILE = 8
LANES = 128
GROUP = 2
NEAR = 4


def tables(bins):
    lag_total = 2 * bins
    lag = np.arange(lag_total)[:, None]
    freq = np.arange(bins)[None, :]
    theta = (lag * freq % lag_total) * (2.0 * math.pi / lag_total)
    cosine, sine = np.cos(theta), np.sin(theta)
    inverse = np.concatenate(
        [np.concatenate([cosine, -sine], 1), np.concatenate([sine, cosine], 1)], 0
    ) / math.sqrt(bins)
    forward = np.concatenate([cosine, -sine], 1) / math.sqrt(lag_total)
    return (
        inverse.astype(np.float32).astype(jnp.bfloat16),
        forward.astype(np.float32).astype(jnp.bfloat16),
    )


def cos_sin(steps):
    quarter = PERIOD // 4
    place = steps & (PERIOD - 1)
    quadrant = (place + quarter // 2) // quarter
    x = (place - quadrant * quarter).astype(jnp.float32) * (2.0 * math.pi / PERIOD)
    y = x * x
    sine = x * (1.0 + y * (-1.0 / 6 + y * (1.0 / 120 - y * (1.0 / 5040))))
    cosine = 1.0 + y * (-0.5 + y * (1.0 / 24 + y * (-1.0 / 720 + y * (1.0 / 40320))))
    odd = (quadrant & 1) == 1
    first = jnp.where(odd, sine, cosine)
    second = jnp.where(odd, cosine, sine)
    first = jnp.where(((quadrant + 1) & 2) == 2, -first, first)
    second = jnp.where((quadrant & 2) == 2, -second, second)
    return first, second


def exchange(source, target, send_sem, recv_sem, day, chan):
    return pltpu.make_async_remote_copy(
        src_ref=source,
        dst_ref=target,
        send_sem=send_sem,
        recv_sem=recv_sem,
        device_id={"days": day, "chan": chan},
        device_id_type=pl.DeviceIdType.MESH,
    )


def pack_halves(spectra_ref, kept, sent, day):
    count, depth, width = spectra_ref.shape
    half = width // 2
    left = lax.broadcasted_iota(jnp.int32, (depth, width), 1) < half
    upper = jnp.full((depth, width), day, jnp.int32) == 1
    for pair in range(count // 2):
        first = spectra_ref[2 * pair].astype(jnp.float32)
        second = spectra_ref[2 * pair + 1].astype(jnp.float32)
        lows = jnp.where(left, first, pltpu.roll(second, half, 1))
        highs = jnp.where(left, pltpu.roll(first, half, 1), second)
        kept[pair] = jnp.where(upper, highs, lows).astype(jnp.bfloat16)
        sent[pair] = jnp.where(upper, lows, highs).astype(jnp.bfloat16)


def source_columns(spectra_ref, sources_ref, chan):
    count, depth, width = spectra_ref.shape
    shape = (count * NSRC, width)
    row = lax.broadcasted_iota(jnp.int32, shape, 0)
    channel = lax.broadcasted_iota(jnp.int32, shape, 1) + chan * width
    wanted = jnp.zeros(shape, jnp.int32)
    for s in range(NSRC):
        wanted = jnp.where(row % NSRC == s, sources_ref[s], wanted)
    total = 0.0
    for w in range(count):
        pick = ((channel == wanted) & (row // NSRC == w)).astype(jnp.float32).astype(jnp.bfloat16)
        total = total + lax.dot_general(
            pick, spectra_ref[w], (((1,), (1,)), ((), ())), preferred_element_type=jnp.float32
        )
    return total.astype(jnp.bfloat16)


def correlate(x_ref, source_rows, inverse_ref, analytic, first_slot):
    pairs, depth, width = x_ref.shape
    bins, half = depth // 2, width // 2
    wide = NSRC * width
    shape = (source_rows.shape[0], wide)
    rows = lax.broadcasted_iota(jnp.int32, shape, 0)
    lane = lax.broadcasted_iota(jnp.int32, shape, 1)
    for pair in range(pairs):
        wanted = (2 * pair + lane % width // half) * NSRC + lane // width
        pick = (rows == wanted).astype(jnp.float32).astype(jnp.bfloat16)
        source = lax.dot_general(
            source_rows, pick, (((0,), (0,)), ((), ())), preferred_element_type=jnp.float32
        )
        channel = x_ref[pair].astype(jnp.float32)
        channel = jnp.concatenate([channel] * NSRC, 1)
        real_s, imag_s = source[:bins], source[bins:]
        real_x, imag_x = channel[:bins], channel[bins:]
        product = jnp.concatenate(
            [real_s * real_x + imag_s * imag_x, real_s * imag_x - imag_s * real_x], 0
        ).astype(jnp.bfloat16)
        analytic[first_slot + pair] = jnp.dot(
            inverse_ref[...], product, preferred_element_type=jnp.float32
        )


def stacks(analytic, weighted, forward_ref, spectrum, windows):
    slots, depth, wide = analytic.shape
    lags, width = depth // 2, wide // NSRC
    half = width // 2
    block = 16

    def stack(step, carry):
        start = pl.multiple_of(step * block, block)
        linear = phase_re = phase_im = 0.0
        for slot in range(slots):
            corr = analytic[slot, pl.ds(start, block)]
            hilb = analytic[slot, pl.ds(lags + start, block)]
            over = jnp.minimum(lax.rsqrt(corr * corr + hilb * hilb), 2.0)
            linear = linear + corr
            phase_re = phase_re + corr * over
            phase_im = phase_im + hilb * over

        def fold(value):
            parts = []
            for s in range(NSRC):
                part = value[:, s * width : (s + 1) * width]
                parts.append(part + pltpu.roll(part, half, 1))
            side = lax.broadcasted_iota(jnp.int32, (block, width), 1) < half
            return jnp.where(side, parts[0], parts[1])

        linear, phase_re, phase_im = fold(linear), fold(phase_re), fold(phase_im)
        result = linear * (phase_re * phase_re + phase_im * phase_im) * (1.0 / windows**3)
        weighted[pl.ds(start, block)] = result.astype(jnp.bfloat16)
        return carry

    lax.fori_loop(0, lags // block, stack, 0)
    result = lax.dot_general(
        weighted[...], forward_ref[...], (((0,), (0,)), ((), ())), preferred_element_type=jnp.float32
    )
    for part in range(lags // LANES):
        spectrum[part] = result[:, part * LANES : (part + 1) * LANES]


def slant(offset_ref, spectrum, base, sums, half, bins, scaling, part):
    sums[part] = jnp.zeros(sums.shape[1:], jnp.float32)
    steps = NSLOW // TILE
    low = lax.broadcasted_iota(jnp.int32, (TILE, LANES), 0)
    freq = lax.broadcasted_iota(jnp.int32, (TILE, LANES), 1) + part * LANES
    product = low * freq
    part_im = bins // LANES + part

    def group(number, carry):
        now, before, twice = [], [], []
        for member in range(GROUP):
            channel = number * GROUP + member
            offset = offset_ref[base + channel]
            jump_cos, jump_sin = cos_sin(freq * (offset * TILE))
            cosine, sine = cos_sin(product * offset)
            back_cos = cosine * jump_cos + sine * jump_sin
            back_sin = sine * jump_cos - cosine * jump_sin
            twice.append(2.0 * jump_cos)
            for s in range(NSRC):
                row = pl.ds(s * half + channel, 1)
                real = spectrum[part, row] * scaling
                imag = spectrum[part_im, row] * scaling
                now.append([real * cosine - imag * sine, real * sine + imag * cosine])
                before.append([real * back_cos - imag * back_sin, real * back_sin + imag * back_cos])
        for step in range(steps):
            for s in range(NSRC):
                for piece in range(2):
                    total = now[s][piece]
                    for member in range(1, GROUP):
                        total = total + now[member * NSRC + s][piece]
                    here = (part, s, piece, pl.ds(step * TILE, TILE))
                    sums[here] = sums[here] + total
            if step + 1 < steps:
                for member in range(GROUP):
                    for s in range(NSRC):
                        at = member * NSRC + s
                        for piece in range(2):
                            later = twice[member] * now[at][piece] - before[at][piece]
                            before[at][piece] = now[at][piece]
                            now[at][piece] = later
        return carry

    lax.fori_loop(0, half // GROUP, group, 0)


def kernel(
    windows, scaling, days, chans, spectra_ref, sources_ref, offset_ref, inverse_hbm, forward_hbm, out_ref,
    kept, sent, got, column, columns_far, plane, columns_near, analytic, weighted, spectrum, sums,
    leaving, arriving, owned, landing, inverse_ref, forward_ref, table_sem,
    half_sem, far_sem, near_sem, leave_sem, own_sem,
):
    count, depth, width = spectra_ref.shape
    bins, half = depth // 2, width // 2
    parts = bins // LANES
    far = chans // NEAR
    rows = NSLOW // chans
    day, chan = lax.axis_index("days"), lax.axis_index("chan")
    high, low = chan // NEAR, chan % NEAR
    table_copies = [
        pltpu.make_async_copy(inverse_hbm, inverse_ref, table_sem.at[0]),
        pltpu.make_async_copy(forward_hbm, forward_ref, table_sem.at[1]),
    ]
    for copy in table_copies:
        copy.start()

    near_peers = [
        (dd, dl, (day + dd) % days, (low + dl) % NEAR)
        for dd in range(days)
        for dl in range(NEAR)
        if dd or dl
    ]
    far_peers = [
        (dd, dh, (day + dd) % days, (high + dh) % far)
        for dd in range(days)
        for dh in range(far)
        if dd or dh
    ]
    barrier = pltpu.get_barrier_semaphore()
    greeted = 0
    for dd, dl, to_day, to_low in near_peers:
        pl.semaphore_signal(
            barrier, inc=1, device_id={"days": to_day, "chan": high * NEAR + to_low},
            device_id_type=pl.DeviceIdType.MESH,
        )
        greeted += 1
    for dd, dh, to_day, to_high in far_peers:
        if dh:
            pl.semaphore_signal(
                barrier, inc=1, device_id={"days": to_day, "chan": to_high * NEAR + low},
                device_id_type=pl.DeviceIdType.MESH,
            )
            greeted += 1
    column[...] = source_columns(spectra_ref, sources_ref, chan)
    pack_halves(spectra_ref, kept, sent, day)
    pl.semaphore_wait(barrier, greeted)

    far_copies = []
    for dd, dh, to_day, to_high in far_peers:
        if dd == 0:
            copy = exchange(
                column, columns_far.at[dh - 1], far_sem.at[0, dh - 1], far_sem.at[1, dh - 1],
                day, to_high * NEAR + low,
            )
            copy.start()
            far_copies.append(copy)
    half_copy = exchange(sent, got, half_sem.at[0], half_sem.at[1], (day + 1) % days, chan)
    half_copy.start()
    total = column[...].astype(jnp.float32)
    for index, copy in enumerate(far_copies):
        copy.wait_recv()
        total = total + columns_far[index].astype(jnp.float32)
    plane[...] = total.astype(jnp.bfloat16)
    near_copies = []
    for index, (dd, dl, to_day, to_low) in enumerate(near_peers):
        copy = exchange(
            plane, columns_near.at[index], near_sem.at[0, index], near_sem.at[1, index],
            to_day, high * NEAR + to_low,
        )
        copy.start()
        near_copies.append((dd, copy))

    def gather(wanted, value):
        for index, (dd, copy) in enumerate(near_copies):
            if dd == wanted:
                copy.wait_recv()
                value = value + columns_near[index].astype(jnp.float32)
        return value.astype(jnp.bfloat16)

    pairs = count // 2
    rows_own = gather(0, total)
    for copy in table_copies:
        copy.wait()
    correlate(kept, rows_own, inverse_ref, analytic, 0)
    rows_other = gather(1, 0.0)
    half_copy.wait_recv()
    correlate(got, rows_other, inverse_ref, analytic, pairs)
    stacks(analytic, weighted, forward_ref, spectrum, windows)

    leave_copies = []
    wire = leaving.dtype
    for part in range(parts):
        slant(offset_ref, spectrum, day * half, sums, half, bins, scaling, part)
        for lo in range(NEAR):
            for s in range(NSRC):
                for hi in range(far):
                    first = (hi * NEAR + lo) * rows
                    leaving[part, lo, s, :, hi * rows : (hi + 1) * rows] = sums[
                        part, s, :, first : first + rows
                    ].astype(wire)
        for index, (dd, dl, to_day, to_low) in enumerate(near_peers):
            copy = exchange(
                leaving.at[part, to_low, to_day], arriving.at[part, index],
                leave_sem.at[0, part, index], leave_sem.at[1, part, index],
                to_day, high * NEAR + to_low,
            )
            copy.start()
            leave_copies.append((part, index, copy))
    for part in range(parts):
        total = leaving[part, low, day].astype(jnp.float32)
        for at, index, copy in leave_copies:
            if at == part:
                copy.wait_recv()
                total = total + arriving[part, index].astype(jnp.float32)
        for hi in range(far):
            owned[hi, part] = total[:, hi * rows : (hi + 1) * rows].astype(wire)
    own_copies = []
    for index, (dd, dh, to_day, to_high) in enumerate(far_peers):
        copy = exchange(
            owned.at[to_high], landing.at[index], own_sem.at[0, index], own_sem.at[1, index],
            to_day, to_high * NEAR + low,
        )
        copy.start()
        own_copies.append((dd, index, copy))
    for shift in range(days):
        total = owned[high].astype(jnp.float32) if shift == 0 else 0.0
        for dd, index, copy in own_copies:
            if dd == shift:
                copy.wait_recv()
                total = total + landing[index].astype(jnp.float32)
        for part in range(parts):
            out_ref[(day + shift) % days, :, :, part * LANES : (part + 1) * LANES] = total[part]
    half_copy.wait_send()
    for copy in far_copies:
        copy.wait_send()
    for dd, copy in near_copies:
        copy.wait_send()
    for part, index, copy in leave_copies:
        copy.wait_send()
    for dd, index, copy in own_copies:
        copy.wait_send()


def shards(spectra, sources, offsets):
    count, depth, width = spectra.shape
    bins, half = depth // 2, width // 2
    days, chans = lax.axis_size("days"), lax.axis_size("chan")
    windows = count * days
    inverse, forward = tables(bins)
    scaling = windows**1.5 / math.sqrt(width * chans)
    far, rows, parts, pairs = chans // NEAR, NSLOW // chans, bins // LANES, count // 2
    near_count, far_count = days * NEAR - 1, days * far - 1
    wire = jnp.bfloat16 if rows % TILE == 0 else jnp.float32
    vmem = pl.BlockSpec(memory_space=pltpu.VMEM)
    smem = pl.BlockSpec(memory_space=pltpu.SMEM)
    anywhere = pl.BlockSpec(memory_space=pl.ANY)
    bf16, f32 = jnp.bfloat16, jnp.float32
    dma = pltpu.SemaphoreType.DMA
    out = pl.pallas_call(
        functools.partial(kernel, windows, scaling, days, chans),
        out_shape=jax.ShapeDtypeStruct((NSRC, 2, rows, bins), f32),
        in_specs=[vmem, smem, smem, anywhere, anywhere],
        out_specs=vmem,
        scratch_shapes=[
            pltpu.VMEM((pairs, depth, width), bf16),
            pltpu.VMEM((pairs, depth, width), bf16),
            pltpu.VMEM((pairs, depth, width), bf16),
            pltpu.VMEM((count * NSRC, depth), bf16),
            pltpu.VMEM((far - 1, count * NSRC, depth), bf16),
            pltpu.VMEM((count * NSRC, depth), bf16),
            pltpu.VMEM((near_count, count * NSRC, depth), bf16),
            pltpu.VMEM((2 * pairs, 2 * depth, NSRC * width), f32),
            pltpu.VMEM((depth, width), bf16),
            pltpu.VMEM((depth // LANES, NSRC * half, LANES), f32),
            pltpu.VMEM((parts, NSRC, 2, NSLOW, LANES), f32),
            pltpu.VMEM((parts, NEAR, NSRC, 2, far * rows, LANES), wire),
            pltpu.VMEM((parts, near_count, 2, far * rows, LANES), wire),
            pltpu.VMEM((far, parts, 2, rows, LANES), wire),
            pltpu.VMEM((far_count, parts, 2, rows, LANES), wire),
            pltpu.VMEM(inverse.shape, bf16),
            pltpu.VMEM(forward.shape, bf16),
            dma((2,)),
            dma((2,)),
            dma((2, far - 1)),
            dma((2, near_count)),
            dma((2, parts, near_count)),
            dma((2, far_count)),
        ],
        compiler_params=pltpu.CompilerParams(collective_id=0, has_side_effects=True),
    )(spectra, sources, offsets, jnp.asarray(inverse), jnp.asarray(forward))
    return out.transpose(2, 0, 1, 3)


def solution(mesh):
    placed = (P("days", None, "chan"), P(), P("chan"))
    return jax.shard_map(
        shards, mesh=mesh, in_specs=placed, out_specs=P("chan", None, None, None), check_vma=False
    )
```

```python
import functools
import math

import jax
import jax.numpy as jnp
import numpy as np
from jax import lax
from jax.experimental import pallas as pl
from jax.experimental.pallas import tpu as pltpu
from jax.sharding import PartitionSpec as P

NSLOW = 128
NSRC = 2
PERIOD = 4096
TILE = 8
LANES = 128
GROUP = 2
NEAR = 4


def tables(bins):
    lag_total = 2 * bins
    lag = np.arange(lag_total)[:, None]
    freq = np.arange(bins)[None, :]
    theta = (lag * freq % lag_total) * (2.0 * math.pi / lag_total)
    cosine, sine = np.cos(theta), np.sin(theta)
    inverse = np.concatenate(
        [np.concatenate([cosine, -sine], 1), np.concatenate([sine, cosine], 1)], 0
    ) / math.sqrt(bins)
    forward = np.concatenate([cosine, -sine], 1) / math.sqrt(lag_total)
    return (
        inverse.astype(np.float32).astype(jnp.bfloat16),
        forward.astype(np.float32).astype(jnp.bfloat16),
    )


def cos_sin(steps):
    quarter = PERIOD // 4
    place = steps & (PERIOD - 1)
    quadrant = (place + quarter // 2) // quarter
    x = (place - quadrant * quarter).astype(jnp.float32) * (2.0 * math.pi / PERIOD)
    y = x * x
    sine = x * (1.0 + y * (-1.0 / 6 + y * (1.0 / 120 - y * (1.0 / 5040))))
    cosine = 1.0 + y * (-0.5 + y * (1.0 / 24 + y * (-1.0 / 720 + y * (1.0 / 40320))))
    odd = (quadrant & 1) == 1
    first = jnp.where(odd, sine, cosine)
    second = jnp.where(odd, cosine, sine)
    first = jnp.where(((quadrant + 1) & 2) == 2, -first, first)
    second = jnp.where((quadrant & 2) == 2, -second, second)
    return first, second


def exchange(source, target, send_sem, recv_sem, day, chan):
    return pltpu.make_async_remote_copy(
        src_ref=source,
        dst_ref=target,
        send_sem=send_sem,
        recv_sem=recv_sem,
        device_id={"days": day, "chan": chan},
        device_id_type=pl.DeviceIdType.MESH,
    )


def pack_halves(spectra_ref, kept, sent, day):
    count, depth, width = spectra_ref.shape
    half = width // 2
    left = lax.broadcasted_iota(jnp.int32, (depth, width), 1) < half
    upper = jnp.full((depth, width), day, jnp.int32) == 1
    for pair in range(count // 2):
        first = spectra_ref[2 * pair].astype(jnp.float32)
        second = spectra_ref[2 * pair + 1].astype(jnp.float32)
        lows = jnp.where(left, first, pltpu.roll(second, half, 1))
        highs = jnp.where(left, pltpu.roll(first, half, 1), second)
        kept[pair] = jnp.where(upper, highs, lows).astype(jnp.bfloat16)
        sent[pair] = jnp.where(upper, lows, highs).astype(jnp.bfloat16)


def source_columns(spectra_ref, sources_ref, chan):
    count, depth, width = spectra_ref.shape
    shape = (count * NSRC, width)
    row = lax.broadcasted_iota(jnp.int32, shape, 0)
    channel = lax.broadcasted_iota(jnp.int32, shape, 1) + chan * width
    wanted = jnp.zeros(shape, jnp.int32)
    for s in range(NSRC):
        wanted = jnp.where(row % NSRC == s, sources_ref[s], wanted)
    total = 0.0
    for w in range(count):
        pick = ((channel == wanted) & (row // NSRC == w)).astype(jnp.float32).astype(jnp.bfloat16)
        total = total + lax.dot_general(
            pick, spectra_ref[w], (((1,), (1,)), ((), ())), preferred_element_type=jnp.float32
        )
    return total.astype(jnp.bfloat16)


def correlate(x_ref, source_rows, inverse_ref, analytic, first_slot):
    pairs, depth, width = x_ref.shape
    bins, half = depth // 2, width // 2
    wide = NSRC * width
    shape = (source_rows.shape[0], wide)
    rows = lax.broadcasted_iota(jnp.int32, shape, 0)
    lane = lax.broadcasted_iota(jnp.int32, shape, 1)
    for pair in range(pairs):
        wanted = (2 * pair + lane % width // half) * NSRC + lane // width
        pick = (rows == wanted).astype(jnp.float32).astype(jnp.bfloat16)
        source = lax.dot_general(
            source_rows, pick, (((0,), (0,)), ((), ())), preferred_element_type=jnp.float32
        )
        channel = x_ref[pair].astype(jnp.float32)
        channel = jnp.concatenate([channel] * NSRC, 1)
        real_s, imag_s = source[:bins], source[bins:]
        real_x, imag_x = channel[:bins], channel[bins:]
        product = jnp.concatenate(
            [real_s * real_x + imag_s * imag_x, real_s * imag_x - imag_s * real_x], 0
        ).astype(jnp.bfloat16)
        analytic[first_slot + pair] = jnp.dot(
            inverse_ref[...], product, preferred_element_type=jnp.float32
        )


def stacks(analytic, weighted, forward_ref, spectrum, factor):
    slots, depth, wide = analytic.shape
    lags, width = depth // 2, wide // NSRC
    half = width // 2
    block = 16

    def stack(step, carry):
        start = pl.multiple_of(step * block, block)
        linear = phase_re = phase_im = 0.0
        for slot in range(slots):
            corr = analytic[slot, pl.ds(start, block)]
            hilb = analytic[slot, pl.ds(lags + start, block)]
            over = jnp.minimum(lax.rsqrt(corr * corr + hilb * hilb), 2.0)
            linear = linear + corr
            phase_re = phase_re + corr * over
            phase_im = phase_im + hilb * over

        def fold(value):
            parts = []
            for s in range(NSRC):
                part = value[:, s * width : (s + 1) * width]
                parts.append(part + pltpu.roll(part, half, 1))
            side = lax.broadcasted_iota(jnp.int32, (block, width), 1) < half
            return jnp.where(side, parts[0], parts[1])

        linear, phase_re, phase_im = fold(linear), fold(phase_re), fold(phase_im)
        result = linear * (phase_re * phase_re + phase_im * phase_im) * factor
        weighted[pl.ds(start, block)] = result.astype(jnp.bfloat16)
        return carry

    lax.fori_loop(0, lags // block, stack, 0, unroll=4)
    result = lax.dot_general(
        weighted[...], forward_ref[...], (((0,), (0,)), ((), ())), preferred_element_type=jnp.float32
    )
    for part in range(lags // LANES):
        spectrum[part] = result[:, part * LANES : (part + 1) * LANES]


def phase_tables(offset_ref, base, phases, half, part):
    low = lax.broadcasted_iota(jnp.int32, (TILE, LANES), 0)
    freq = lax.broadcasted_iota(jnp.int32, (TILE, LANES), 1) + part * LANES
    product = low * freq

    def group(number, carry):
        for member in range(GROUP):
            channel = number * GROUP + member
            offset = offset_ref[base + channel]
            jump_cos, jump_sin = cos_sin(freq * (offset * TILE))
            cosine, sine = cos_sin(product * offset)
            phases[part, channel, 0] = cosine
            phases[part, channel, 1] = sine
            phases[part, channel, 2] = cosine * jump_cos + sine * jump_sin
            phases[part, channel, 3] = sine * jump_cos - cosine * jump_sin
            phases[part, channel, 4] = 2.0 * jump_cos
        return carry

    lax.fori_loop(0, half // GROUP, group, 0)


def slant(phases, spectrum, sums, half, bins, part):
    sums[part] = jnp.zeros(sums.shape[1:], jnp.float32)
    steps = NSLOW // TILE
    part_im = bins // LANES + part

    def group(number, carry):
        now, before, twice = [], [], []
        for member in range(GROUP):
            channel = number * GROUP + member
            cosine, sine = phases[part, channel, 0], phases[part, channel, 1]
            back_cos, back_sin = phases[part, channel, 2], phases[part, channel, 3]
            twice.append(phases[part, channel, 4])
            for s in range(NSRC):
                row = pl.ds(s * half + channel, 1)
                real, imag = spectrum[part, row], spectrum[part_im, row]
                now.append([real * cosine - imag * sine, real * sine + imag * cosine])
                before.append([real * back_cos - imag * back_sin, real * back_sin + imag * back_cos])
        for step in range(steps):
            for s in range(NSRC):
                for piece in range(2):
                    total = now[s][piece]
                    for member in range(1, GROUP):
                        total = total + now[member * NSRC + s][piece]
                    here = (part, s, piece, pl.ds(step * TILE, TILE))
                    sums[here] = sums[here] + total
            if step + 1 < steps:
                for member in range(GROUP):
                    for s in range(NSRC):
                        at = member * NSRC + s
                        for piece in range(2):
                            later = twice[member] * now[at][piece] - before[at][piece]
                            before[at][piece] = now[at][piece]
                            now[at][piece] = later
        return carry

    lax.fori_loop(0, half // GROUP, group, 0)


def kernel(
    windows, scaling, days, chans, spectra_ref, sources_ref, offset_ref, inverse_hbm, forward_hbm, out_ref,
    kept, sent, got, column, columns_far, plane, columns_near, analytic, weighted, spectrum, sums, phases,
    leaving, arriving, owned, landing, inverse_ref, forward_ref, table_sem,
    half_sem, far_sem, near_sem, leave_sem, own_sem,
):
    count, depth, width = spectra_ref.shape
    bins, half = depth // 2, width // 2
    parts = bins // LANES
    far = chans // NEAR
    rows = NSLOW // chans
    day, chan = lax.axis_index("days"), lax.axis_index("chan")
    high, low = chan // NEAR, chan % NEAR
    table_copies = [
        pltpu.make_async_copy(inverse_hbm, inverse_ref, table_sem.at[0]),
        pltpu.make_async_copy(forward_hbm, forward_ref, table_sem.at[1]),
    ]
    for copy in table_copies:
        copy.start()

    near_peers = [
        (dd, dl, (day + dd) % days, (low + dl) % NEAR)
        for dd in range(days)
        for dl in range(NEAR)
        if dd or dl
    ]
    far_peers = [
        (dd, dh, (day + dd) % days, (high + dh) % far)
        for dd in range(days)
        for dh in range(far)
        if dd or dh
    ]
    barrier = pltpu.get_barrier_semaphore()
    greeted = 0
    for dd, dl, to_day, to_low in near_peers:
        pl.semaphore_signal(
            barrier, inc=1, device_id={"days": to_day, "chan": high * NEAR + to_low},
            device_id_type=pl.DeviceIdType.MESH,
        )
        greeted += 1
    for dd, dh, to_day, to_high in far_peers:
        if dh:
            pl.semaphore_signal(
                barrier, inc=1, device_id={"days": to_day, "chan": to_high * NEAR + low},
                device_id_type=pl.DeviceIdType.MESH,
            )
            greeted += 1
    column[...] = source_columns(spectra_ref, sources_ref, chan)
    pack_halves(spectra_ref, kept, sent, day)
    pl.semaphore_wait(barrier, greeted)

    far_copies = []
    for dd, dh, to_day, to_high in far_peers:
        if dd == 0:
            copy = exchange(
                column, columns_far.at[dh - 1], far_sem.at[0, dh - 1], far_sem.at[1, dh - 1],
                day, to_high * NEAR + low,
            )
            copy.start()
            far_copies.append(copy)
    half_copy = exchange(sent, got, half_sem.at[0], half_sem.at[1], (day + 1) % days, chan)
    half_copy.start()
    phase_tables(offset_ref, day * half, phases, half, 0)
    total = column[...].astype(jnp.float32)
    for index, copy in enumerate(far_copies):
        copy.wait_recv()
        total = total + columns_far[index].astype(jnp.float32)
    plane[...] = total.astype(jnp.bfloat16)
    near_copies = []
    for index, (dd, dl, to_day, to_low) in enumerate(near_peers):
        copy = exchange(
            plane, columns_near.at[index], near_sem.at[0, index], near_sem.at[1, index],
            to_day, high * NEAR + to_low,
        )
        copy.start()
        near_copies.append((dd, copy))
    for part in range(1, parts):
        phase_tables(offset_ref, day * half, phases, half, part)

    def gather(wanted, value):
        for index, (dd, copy) in enumerate(near_copies):
            if dd == wanted:
                copy.wait_recv()
                value = value + columns_near[index].astype(jnp.float32)
        return value.astype(jnp.bfloat16)

    pairs = count // 2
    rows_own = gather(0, total)
    for copy in table_copies:
        copy.wait()
    correlate(kept, rows_own, inverse_ref, analytic, 0)
    rows_other = gather(1, 0.0)
    half_copy.wait_recv()
    correlate(got, rows_other, inverse_ref, analytic, pairs)
    stacks(analytic, weighted, forward_ref, spectrum, scaling / windows**3)

    leave_copies = []
    wire = leaving.dtype
    for part in range(parts):
        slant(phases, spectrum, sums, half, bins, part)
        for lo in range(NEAR):
            for s in range(NSRC):
                for hi in range(far):
                    first = (hi * NEAR + lo) * rows
                    leaving[part, lo, s, :, hi * rows : (hi + 1) * rows] = sums[
                        part, s, :, first : first + rows
                    ].astype(wire)
        for index, (dd, dl, to_day, to_low) in enumerate(near_peers):
            copy = exchange(
                leaving.at[part, to_low, to_day], arriving.at[part, index],
                leave_sem.at[0, part, index], leave_sem.at[1, part, index],
                to_day, high * NEAR + to_low,
            )
            copy.start()
            leave_copies.append((part, index, copy))
    for part in range(parts):
        total = leaving[part, low, day].astype(jnp.float32)
        for at, index, copy in leave_copies:
            if at == part:
                copy.wait_recv()
                total = total + arriving[part, index].astype(jnp.float32)
        for hi in range(far):
            owned[hi, part] = total[:, hi * rows : (hi + 1) * rows].astype(wire)
    own_copies = []
    for index, (dd, dh, to_day, to_high) in enumerate(far_peers):
        copy = exchange(
            owned.at[to_high], landing.at[index], own_sem.at[0, index], own_sem.at[1, index],
            to_day, to_high * NEAR + low,
        )
        copy.start()
        own_copies.append((dd, index, copy))
    for shift in range(days):
        total = owned[high].astype(jnp.float32) if shift == 0 else 0.0
        for dd, index, copy in own_copies:
            if dd == shift:
                copy.wait_recv()
                total = total + landing[index].astype(jnp.float32)
        for part in range(parts):
            for piece in range(2):
                out_ref[:, (day + shift) % days, piece, part * LANES : (part + 1) * LANES] = total[part, piece]
    half_copy.wait_send()
    for copy in far_copies:
        copy.wait_send()
    for dd, copy in near_copies:
        copy.wait_send()
    for part, index, copy in leave_copies:
        copy.wait_send()
    for dd, index, copy in own_copies:
        copy.wait_send()


def shards(spectra, sources, offsets):
    count, depth, width = spectra.shape
    bins, half = depth // 2, width // 2
    days, chans = lax.axis_size("days"), lax.axis_size("chan")
    windows = count * days
    inverse, forward = tables(bins)
    scaling = windows**1.5 / math.sqrt(width * chans)
    far, rows, parts, pairs = chans // NEAR, NSLOW // chans, bins // LANES, count // 2
    near_count, far_count = days * NEAR - 1, days * far - 1
    wire = jnp.bfloat16 if rows % TILE == 0 else jnp.float32
    vmem = pl.BlockSpec(memory_space=pltpu.VMEM)
    smem = pl.BlockSpec(memory_space=pltpu.SMEM)
    anywhere = pl.BlockSpec(memory_space=pl.ANY)
    bf16, f32 = jnp.bfloat16, jnp.float32
    dma = pltpu.SemaphoreType.DMA
    return pl.pallas_call(
        functools.partial(kernel, windows, scaling, days, chans),
        out_shape=jax.ShapeDtypeStruct((rows, NSRC, 2, bins), f32),
        in_specs=[vmem, smem, smem, anywhere, anywhere],
        out_specs=vmem,
        scratch_shapes=[
            pltpu.VMEM((pairs, depth, width), bf16),
            pltpu.VMEM((pairs, depth, width), bf16),
            pltpu.VMEM((pairs, depth, width), bf16),
            pltpu.VMEM((count * NSRC, depth), bf16),
            pltpu.VMEM((far - 1, count * NSRC, depth), bf16),
            pltpu.VMEM((count * NSRC, depth), bf16),
            pltpu.VMEM((near_count, count * NSRC, depth), bf16),
            pltpu.VMEM((2 * pairs, 2 * depth, NSRC * width), f32),
            pltpu.VMEM((depth, width), bf16),
            pltpu.VMEM((depth // LANES, NSRC * half, LANES), f32),
            pltpu.VMEM((parts, NSRC, 2, NSLOW, LANES), f32),
            pltpu.VMEM((parts, half, 5, TILE, LANES), f32),
            pltpu.VMEM((parts, NEAR, NSRC, 2, far * rows, LANES), wire),
            pltpu.VMEM((parts, near_count, 2, far * rows, LANES), wire),
            pltpu.VMEM((far, parts, 2, rows, LANES), wire),
            pltpu.VMEM((far_count, parts, 2, rows, LANES), wire),
            pltpu.VMEM(inverse.shape, bf16),
            pltpu.VMEM(forward.shape, bf16),
            dma((2,)),
            dma((2,)),
            dma((2, far - 1)),
            dma((2, near_count)),
            dma((2, parts, near_count)),
            dma((2, far_count)),
        ],
        compiler_params=pltpu.CompilerParams(collective_id=0, has_side_effects=True),
    )(spectra, sources, offsets, jnp.asarray(inverse), jnp.asarray(forward))


def solution(mesh):
    placed = (P("days", None, "chan"), P(), P("chan"))
    return jax.shard_map(
        shards, mesh=mesh, in_specs=placed, out_specs=P("chan", None, None, None), check_vma=False
    )
```

```python
import functools
import math

import jax
import jax.numpy as jnp
import numpy as np
from jax import lax
from jax.experimental import pallas as pl
from jax.experimental.pallas import tpu as pltpu
from jax.sharding import PartitionSpec as P

NSLOW = 128
NSRC = 2
PERIOD = 4096
TILE = 8
LANES = 128
GROUP = 2
SLANT_GROUP = 4
NEAR = 4


def tables(bins):
    lag_total = 2 * bins
    lag = np.arange(lag_total)[:, None]
    freq = np.arange(bins)[None, :]
    theta = (lag * freq % lag_total) * (2.0 * math.pi / lag_total)
    cosine, sine = np.cos(theta), np.sin(theta)
    inverse = np.concatenate(
        [np.concatenate([cosine, -sine], 1), np.concatenate([sine, cosine], 1)], 0
    ) / math.sqrt(bins)
    forward = np.concatenate([cosine, -sine], 1) / math.sqrt(lag_total)
    return (
        inverse.astype(np.float32).astype(jnp.bfloat16),
        forward.astype(np.float32).astype(jnp.bfloat16),
    )


def cos_sin(steps):
    quarter = PERIOD // 4
    place = steps & (PERIOD - 1)
    quadrant = (place + quarter // 2) // quarter
    x = (place - quadrant * quarter).astype(jnp.float32) * (2.0 * math.pi / PERIOD)
    y = x * x
    sine = x * (1.0 + y * (-1.0 / 6 + y * (1.0 / 120 - y * (1.0 / 5040))))
    cosine = 1.0 + y * (-0.5 + y * (1.0 / 24 + y * (-1.0 / 720 + y * (1.0 / 40320))))
    odd = (quadrant & 1) == 1
    first = jnp.where(odd, sine, cosine)
    second = jnp.where(odd, cosine, sine)
    first = jnp.where(((quadrant + 1) & 2) == 2, -first, first)
    second = jnp.where((quadrant & 2) == 2, -second, second)
    return first, second


def exchange(source, target, send_sem, recv_sem, day, chan):
    return pltpu.make_async_remote_copy(
        src_ref=source,
        dst_ref=target,
        send_sem=send_sem,
        recv_sem=recv_sem,
        device_id={"days": day, "chan": chan},
        device_id_type=pl.DeviceIdType.MESH,
    )


def pack_halves(spectra_ref, kept, sent, day):
    count, depth, width = spectra_ref.shape
    half = width // 2
    left = lax.broadcasted_iota(jnp.int32, (depth, width), 1) < half
    upper = jnp.full((depth, width), day, jnp.int32) == 1
    for pair in range(count // 2):
        first = spectra_ref[2 * pair].astype(jnp.float32)
        second = spectra_ref[2 * pair + 1].astype(jnp.float32)
        lows = jnp.where(left, first, pltpu.roll(second, half, 1))
        highs = jnp.where(left, pltpu.roll(first, half, 1), second)
        kept[pair] = jnp.where(upper, highs, lows).astype(jnp.bfloat16)
        sent[pair] = jnp.where(upper, lows, highs).astype(jnp.bfloat16)


def source_columns(spectra_ref, sources_ref, chan):
    count, depth, width = spectra_ref.shape
    shape = (count * NSRC, width)
    row = lax.broadcasted_iota(jnp.int32, shape, 0)
    channel = lax.broadcasted_iota(jnp.int32, shape, 1) + chan * width
    wanted = jnp.zeros(shape, jnp.int32)
    for s in range(NSRC):
        wanted = jnp.where(row % NSRC == s, sources_ref[s], wanted)
    total = 0.0
    for w in range(count):
        pick = ((channel == wanted) & (row // NSRC == w)).astype(jnp.float32).astype(jnp.bfloat16)
        total = total + lax.dot_general(
            pick, spectra_ref[w], (((1,), (1,)), ((), ())), preferred_element_type=jnp.float32
        )
    return total.astype(jnp.bfloat16)


def correlate(x_ref, source_rows, inverse_ref, analytic, first_slot):
    pairs, depth, width = x_ref.shape
    bins, half = depth // 2, width // 2
    wide = NSRC * width
    shape = (source_rows.shape[0], wide)
    rows = lax.broadcasted_iota(jnp.int32, shape, 0)
    lane = lax.broadcasted_iota(jnp.int32, shape, 1)
    for pair in range(pairs):
        wanted = (2 * pair + lane % width // half) * NSRC + lane // width
        pick = (rows == wanted).astype(jnp.float32).astype(jnp.bfloat16)
        source = lax.dot_general(
            source_rows, pick, (((0,), (0,)), ((), ())), preferred_element_type=jnp.float32
        )
        channel = x_ref[pair].astype(jnp.float32)
        channel = jnp.concatenate([channel] * NSRC, 1)
        real_s, imag_s = source[:bins], source[bins:]
        real_x, imag_x = channel[:bins], channel[bins:]
        product = jnp.concatenate(
            [real_s * real_x + imag_s * imag_x, real_s * imag_x - imag_s * real_x], 0
        ).astype(jnp.bfloat16)
        analytic[first_slot + pair] = jnp.dot(
            inverse_ref[...], product, preferred_element_type=jnp.float32
        )


def stack_sums(analytic, slots, start, block, lags, totals):
    linear, phase_re, phase_im = totals
    for slot in slots:
        corr = analytic[slot, pl.ds(start, block)]
        hilb = analytic[slot, pl.ds(lags + start, block)]
        over = jnp.minimum(lax.rsqrt(corr * corr + hilb * hilb), 2.0)
        linear = linear + corr
        phase_re = phase_re + corr * over
        phase_im = phase_im + hilb * over
    return linear, phase_re, phase_im


def first_stacks(analytic, slots, held):
    lags = analytic.shape[1] // 2
    block = 16

    def stack(step, carry):
        start = pl.multiple_of(step * block, block)
        totals = stack_sums(analytic, slots, start, block, lags, (0.0, 0.0, 0.0))
        for index, total in enumerate(totals):
            held[index, pl.ds(start, block)] = total
        return carry

    lax.fori_loop(0, lags // block, stack, 0, unroll=4)


def last_stacks(analytic, slots, held, weighted, forward_ref, spectrum, factor):
    lags, width = analytic.shape[1] // 2, analytic.shape[2] // NSRC
    half = width // 2
    block = 16

    def stack(step, carry):
        start = pl.multiple_of(step * block, block)
        totals = tuple(held[index, pl.ds(start, block)] for index in range(3))
        totals = stack_sums(analytic, slots, start, block, lags, totals)

        def fold(value):
            parts = []
            for s in range(NSRC):
                part = value[:, s * width : (s + 1) * width]
                parts.append(part + pltpu.roll(part, half, 1))
            side = lax.broadcasted_iota(jnp.int32, (block, width), 1) < half
            return jnp.where(side, parts[0], parts[1])

        linear, phase_re, phase_im = (fold(total) for total in totals)
        result = linear * (phase_re * phase_re + phase_im * phase_im) * factor
        weighted[pl.ds(start, block)] = result.astype(jnp.bfloat16)
        return carry

    lax.fori_loop(0, lags // block, stack, 0, unroll=4)
    result = lax.dot_general(
        weighted[...], forward_ref[...], (((0,), (0,)), ((), ())), preferred_element_type=jnp.float32
    )
    for part in range(lags // LANES):
        spectrum[part] = result[:, part * LANES : (part + 1) * LANES]


def phase_tables(offset_ref, base, phases, half, part):
    low = lax.broadcasted_iota(jnp.int32, (TILE, LANES), 0)
    freq = lax.broadcasted_iota(jnp.int32, (TILE, LANES), 1) + part * LANES
    product = low * freq

    def group(number, carry):
        for member in range(GROUP):
            channel = number * GROUP + member
            offset = offset_ref[base + channel]
            jump_cos, jump_sin = cos_sin(freq * (offset * TILE))
            cosine, sine = cos_sin(product * offset)
            phases[part, channel, 0] = cosine
            phases[part, channel, 1] = sine
            phases[part, channel, 2] = cosine * jump_cos + sine * jump_sin
            phases[part, channel, 3] = sine * jump_cos - cosine * jump_sin
            phases[part, channel, 4] = 2.0 * jump_cos
        return carry

    lax.fori_loop(0, half // GROUP, group, 0)


def slant(phases, spectrum, sums, half, bins, part, source):
    sums[part, source] = jnp.zeros(sums.shape[2:], jnp.float32)
    steps = NSLOW // TILE
    part_im = bins // LANES + part

    def group(number, carry):
        now, before, twice = [], [], []
        for member in range(SLANT_GROUP):
            channel = number * SLANT_GROUP + member
            cosine, sine = phases[part, channel, 0], phases[part, channel, 1]
            back_cos, back_sin = phases[part, channel, 2], phases[part, channel, 3]
            twice.append(phases[part, channel, 4])
            row = pl.ds(source * half + channel, 1)
            real, imag = spectrum[part, row], spectrum[part_im, row]
            now.append([real * cosine - imag * sine, real * sine + imag * cosine])
            before.append([real * back_cos - imag * back_sin, real * back_sin + imag * back_cos])
        for step in range(steps):
            for piece in range(2):
                total = now[0][piece]
                for member in range(1, SLANT_GROUP):
                    total = total + now[member][piece]
                here = (part, source, piece, pl.ds(step * TILE, TILE))
                sums[here] = sums[here] + total
            if step + 1 < steps:
                for member in range(SLANT_GROUP):
                    for piece in range(2):
                        later = twice[member] * now[member][piece] - before[member][piece]
                        before[member][piece] = now[member][piece]
                        now[member][piece] = later
        return carry

    lax.fori_loop(0, half // SLANT_GROUP, group, 0)


def kernel(
    windows, scaling, days, chans, spectra_hbm, sources_ref, offset_ref, inverse_hbm, forward_hbm, out_ref,
    kept, sent, got, column, columns_far, plane, columns_near, analytic, weighted, spectrum, sums, phases, held, spectra_ref,
    leaving, arriving, owned, landing, inverse_ref, forward_ref, table_sem,
    half_sem, far_sem, near_sem, leave_sem, own_sem,
):
    count, depth, width = spectra_ref.shape
    bins, half = depth // 2, width // 2
    parts = bins // LANES
    far = chans // NEAR
    rows = NSLOW // chans
    day, chan = lax.axis_index("days"), lax.axis_index("chan")
    high, low = chan // NEAR, chan % NEAR
    table_copies = [
        pltpu.make_async_copy(inverse_hbm, inverse_ref, table_sem.at[0]),
        pltpu.make_async_copy(forward_hbm, forward_ref, table_sem.at[1]),
    ]
    near_peers = [
        (dd, dl, (day + dd) % days, (low + dl) % NEAR)
        for dd in range(days)
        for dl in range(NEAR)
        if dd or dl
    ]
    far_peers = [
        (dd, dh, (day + dd) % days, (high + dh) % far)
        for dd in range(days)
        for dh in range(far)
        if dd or dh
    ]
    barrier = pltpu.get_barrier_semaphore()
    greeted = 0
    for dd, dl, to_day, to_low in near_peers:
        pl.semaphore_signal(
            barrier, inc=1, device_id={"days": to_day, "chan": high * NEAR + to_low},
            device_id_type=pl.DeviceIdType.MESH,
        )
        greeted += 1
    for dd, dh, to_day, to_high in far_peers:
        if dh:
            pl.semaphore_signal(
                barrier, inc=1, device_id={"days": to_day, "chan": to_high * NEAR + low},
                device_id_type=pl.DeviceIdType.MESH,
            )
            greeted += 1
    spectra_copy = pltpu.make_async_copy(spectra_hbm, spectra_ref, table_sem.at[2])
    spectra_copy.start()
    for copy in table_copies:
        copy.start()
    spectra_copy.wait()
    column[...] = source_columns(spectra_ref, sources_ref, chan)
    pack_halves(spectra_ref, kept, sent, day)
    pl.semaphore_wait(barrier, greeted)

    far_copies = []
    for dd, dh, to_day, to_high in far_peers:
        if dd == 0:
            copy = exchange(
                column, columns_far.at[dh - 1], far_sem.at[0, dh - 1], far_sem.at[1, dh - 1],
                day, to_high * NEAR + low,
            )
            copy.start()
            far_copies.append(copy)
    half_copy = exchange(sent, got, half_sem.at[0], half_sem.at[1], (day + 1) % days, chan)
    half_copy.start()
    phase_tables(offset_ref, day * half, phases, half, 0)
    total = column[...].astype(jnp.float32)
    for index, copy in enumerate(far_copies):
        copy.wait_recv()
        total = total + columns_far[index].astype(jnp.float32)
    plane[...] = total.astype(jnp.bfloat16)
    near_copies = []
    for index, (dd, dl, to_day, to_low) in enumerate(near_peers):
        copy = exchange(
            plane, columns_near.at[index], near_sem.at[0, index], near_sem.at[1, index],
            to_day, high * NEAR + to_low,
        )
        copy.start()
        near_copies.append((dd, copy))
    for part in range(1, parts):
        phase_tables(offset_ref, day * half, phases, half, part)

    def gather(wanted, value):
        for index, (dd, copy) in enumerate(near_copies):
            if dd == wanted:
                copy.wait_recv()
                value = value + columns_near[index].astype(jnp.float32)
        return value.astype(jnp.bfloat16)

    pairs = count // 2
    rows_own = gather(0, total)
    for copy in table_copies:
        copy.wait()
    correlate(kept, rows_own, inverse_ref, analytic, 0)
    first_stacks(analytic, range(pairs), held)
    rows_other = gather(1, 0.0)
    half_copy.wait_recv()
    correlate(got, rows_other, inverse_ref, analytic, pairs)
    others = range(pairs, 2 * pairs)
    last_stacks(analytic, others, held, weighted, forward_ref, spectrum, scaling / windows**3)

    leave_copies = []
    wire = leaving.dtype
    for turn in range(days):
        shift = days - 1 - turn
        target = (day + shift) % days
        for part in range(parts):
            slant(phases, spectrum, sums, half, bins, part, target)
            for lo in range(NEAR):
                for hi in range(far):
                    first = (hi * NEAR + lo) * rows
                    leaving[part, lo, target, :, hi * rows : (hi + 1) * rows] = sums[
                        part, target, :, first : first + rows
                    ].astype(wire)
            for index, (dd, dl, to_day, to_low) in enumerate(near_peers):
                if dd == shift:
                    copy = exchange(
                        leaving.at[part, to_low, target], arriving.at[part, index],
                        leave_sem.at[0, part, index], leave_sem.at[1, part, index],
                        target, high * NEAR + to_low,
                    )
                    copy.start()
                    leave_copies.append((part, index, copy))
    for part in range(parts):
        total = leaving[part, low, day].astype(jnp.float32)
        for at, index, copy in leave_copies:
            if at == part:
                copy.wait_recv()
                total = total + arriving[part, index].astype(jnp.float32)
        for hi in range(far):
            owned[hi, part] = total[:, hi * rows : (hi + 1) * rows].astype(wire)
    own_copies = []
    for index, (dd, dh, to_day, to_high) in enumerate(far_peers):
        copy = exchange(
            owned.at[to_high], landing.at[index], own_sem.at[0, index], own_sem.at[1, index],
            to_day, to_high * NEAR + low,
        )
        copy.start()
        own_copies.append((dd, index, copy))
    for shift in range(days):
        total = owned[high].astype(jnp.float32) if shift == 0 else 0.0
        for dd, index, copy in own_copies:
            if dd == shift:
                copy.wait_recv()
                total = total + landing[index].astype(jnp.float32)
        for part in range(parts):
            for piece in range(2):
                out_ref[:, (day + shift) % days, piece, part * LANES : (part + 1) * LANES] = total[part, piece]
    half_copy.wait_send()
    for copy in far_copies:
        copy.wait_send()
    for dd, copy in near_copies:
        copy.wait_send()
    for part, index, copy in leave_copies:
        copy.wait_send()
    for dd, index, copy in own_copies:
        copy.wait_send()


def shards(spectra, sources, offsets):
    count, depth, width = spectra.shape
    bins, half = depth // 2, width // 2
    days, chans = lax.axis_size("days"), lax.axis_size("chan")
    windows = count * days
    inverse, forward = tables(bins)
    scaling = windows**1.5 / math.sqrt(width * chans)
    far, rows, parts, pairs = chans // NEAR, NSLOW // chans, bins // LANES, count // 2
    near_count, far_count = days * NEAR - 1, days * far - 1
    wire = jnp.bfloat16 if rows % TILE == 0 else jnp.float32
    vmem = pl.BlockSpec(memory_space=pltpu.VMEM)
    smem = pl.BlockSpec(memory_space=pltpu.SMEM)
    anywhere = pl.BlockSpec(memory_space=pl.ANY)
    bf16, f32 = jnp.bfloat16, jnp.float32
    dma = pltpu.SemaphoreType.DMA
    return pl.pallas_call(
        functools.partial(kernel, windows, scaling, days, chans),
        out_shape=jax.ShapeDtypeStruct((rows, NSRC, 2, bins), f32),
        in_specs=[anywhere, smem, smem, anywhere, anywhere],
        out_specs=vmem,
        scratch_shapes=[
            pltpu.VMEM((pairs, depth, width), bf16),
            pltpu.VMEM((pairs, depth, width), bf16),
            pltpu.VMEM((pairs, depth, width), bf16),
            pltpu.VMEM((count * NSRC, depth), bf16),
            pltpu.VMEM((far - 1, count * NSRC, depth), bf16),
            pltpu.VMEM((count * NSRC, depth), bf16),
            pltpu.VMEM((near_count, count * NSRC, depth), bf16),
            pltpu.VMEM((2 * pairs, 2 * depth, NSRC * width), f32),
            pltpu.VMEM((depth, width), bf16),
            pltpu.VMEM((depth // LANES, NSRC * half, LANES), f32),
            pltpu.VMEM((parts, NSRC, 2, NSLOW, LANES), f32),
            pltpu.VMEM((parts, half, 5, TILE, LANES), f32),
            pltpu.VMEM((3, depth, NSRC * width), f32),
            pltpu.VMEM((count, depth, width), bf16),
            pltpu.VMEM((parts, NEAR, NSRC, 2, far * rows, LANES), wire),
            pltpu.VMEM((parts, near_count, 2, far * rows, LANES), wire),
            pltpu.VMEM((far, parts, 2, rows, LANES), wire),
            pltpu.VMEM((far_count, parts, 2, rows, LANES), wire),
            pltpu.VMEM(inverse.shape, bf16),
            pltpu.VMEM(forward.shape, bf16),
            dma((3,)),
            dma((2,)),
            dma((2, far - 1)),
            dma((2, near_count)),
            dma((2, parts, near_count)),
            dma((2, far_count)),
        ],
        compiler_params=pltpu.CompilerParams(collective_id=0, has_side_effects=True),
    )(spectra, sources, offsets, jnp.asarray(inverse), jnp.asarray(forward))


def solution(mesh):
    placed = (P("days", None, "chan"), P(), P("chan"))
    return jax.shard_map(
        shards, mesh=mesh, in_specs=placed, out_specs=P("chan", None, None, None), check_vma=False
    )
```

```python
import functools
import math

import jax
import jax.numpy as jnp
import numpy as np
from jax import lax
from jax.experimental import pallas as pl
from jax.experimental.pallas import tpu as pltpu
from jax.sharding import PartitionSpec as P

NSLOW = 128
NSRC = 2
PERIOD = 4096
TILE = 8
LANES = 128
GROUP = 2
SLANT_GROUP = 4
NEAR = 4


def tables(bins):
    lag_total = 2 * bins
    lag = np.arange(lag_total)[:, None]
    freq = np.arange(bins)[None, :]
    theta = (lag * freq % lag_total) * (2.0 * math.pi / lag_total)
    cosine, sine = np.cos(theta), np.sin(theta)
    inverse = np.concatenate(
        [np.concatenate([cosine, -sine], 1), np.concatenate([sine, cosine], 1)], 0
    ) / math.sqrt(bins)
    forward = np.concatenate([cosine, -sine], 1) / math.sqrt(lag_total)
    return (
        inverse.astype(np.float32).astype(jnp.bfloat16),
        forward.astype(np.float32).astype(jnp.bfloat16),
    )


def cos_sin(steps):
    quarter = PERIOD // 4
    place = steps & (PERIOD - 1)
    quadrant = (place + quarter // 2) // quarter
    x = (place - quadrant * quarter).astype(jnp.float32) * (2.0 * math.pi / PERIOD)
    y = x * x
    sine = x * (1.0 + y * (-1.0 / 6 + y * (1.0 / 120 - y * (1.0 / 5040))))
    cosine = 1.0 + y * (-0.5 + y * (1.0 / 24 + y * (-1.0 / 720 + y * (1.0 / 40320))))
    odd = (quadrant & 1) == 1
    first = jnp.where(odd, sine, cosine)
    second = jnp.where(odd, cosine, sine)
    first = jnp.where(((quadrant + 1) & 2) == 2, -first, first)
    second = jnp.where((quadrant & 2) == 2, -second, second)
    return first, second


def exchange(source, target, send_sem, recv_sem, day, chan):
    return pltpu.make_async_remote_copy(
        src_ref=source,
        dst_ref=target,
        send_sem=send_sem,
        recv_sem=recv_sem,
        device_id={"days": day, "chan": chan},
        device_id_type=pl.DeviceIdType.MESH,
    )


def pack_halves(spectra_ref, kept, sent, day):
    count, depth, width = spectra_ref.shape
    half = width // 2
    left = lax.broadcasted_iota(jnp.int32, (depth, width), 1) < half
    upper = jnp.full((depth, width), day, jnp.int32) == 1
    for pair in range(count // 2):
        first = spectra_ref[2 * pair].astype(jnp.float32)
        second = spectra_ref[2 * pair + 1].astype(jnp.float32)
        lows = jnp.where(left, first, pltpu.roll(second, half, 1))
        highs = jnp.where(left, pltpu.roll(first, half, 1), second)
        kept[pair] = jnp.where(upper, highs, lows).astype(jnp.bfloat16)
        sent[pair] = jnp.where(upper, lows, highs).astype(jnp.bfloat16)


def source_columns(spectra_ref, sources_ref, chan):
    count, depth, width = spectra_ref.shape
    shape = (count * NSRC, width)
    row = lax.broadcasted_iota(jnp.int32, shape, 0)
    channel = lax.broadcasted_iota(jnp.int32, shape, 1) + chan * width
    wanted = jnp.zeros(shape, jnp.int32)
    for s in range(NSRC):
        wanted = jnp.where(row % NSRC == s, sources_ref[s], wanted)
    total = 0.0
    for w in range(count):
        pick = ((channel == wanted) & (row // NSRC == w)).astype(jnp.float32).astype(jnp.bfloat16)
        total = total + lax.dot_general(
            pick, spectra_ref[w], (((1,), (1,)), ((), ())), preferred_element_type=jnp.float32
        )
    return total.astype(jnp.bfloat16)


def correlate(x_ref, source_rows, inverse_ref, analytic, first_slot):
    pairs, depth, width = x_ref.shape
    bins, half = depth // 2, width // 2
    wide = NSRC * width
    shape = (source_rows.shape[0], wide)
    rows = lax.broadcasted_iota(jnp.int32, shape, 0)
    lane = lax.broadcasted_iota(jnp.int32, shape, 1)
    for pair in range(pairs):
        wanted = (2 * pair + lane % width // half) * NSRC + lane // width
        pick = (rows == wanted).astype(jnp.float32).astype(jnp.bfloat16)
        source = lax.dot_general(
            source_rows, pick, (((0,), (0,)), ((), ())), preferred_element_type=jnp.float32
        )
        channel = x_ref[pair].astype(jnp.float32)
        channel = jnp.concatenate([channel] * NSRC, 1)
        real_s, imag_s = source[:bins], source[bins:]
        real_x, imag_x = channel[:bins], channel[bins:]
        product = jnp.concatenate(
            [real_s * real_x + imag_s * imag_x, real_s * imag_x - imag_s * real_x], 0
        ).astype(jnp.bfloat16)
        analytic[first_slot + pair] = jnp.dot(
            inverse_ref[...], product, preferred_element_type=jnp.float32
        )


def stack_sums(analytic, slots, start, block, lags, totals):
    linear, phase_re, phase_im = totals
    for slot in slots:
        corr = analytic[slot, pl.ds(start, block)]
        hilb = analytic[slot, pl.ds(lags + start, block)]
        over = jnp.minimum(lax.rsqrt(corr * corr + hilb * hilb), 2.0)
        linear = linear + corr
        phase_re = phase_re + corr * over
        phase_im = phase_im + hilb * over
    return linear, phase_re, phase_im


def first_stacks(analytic, slots, held):
    lags = analytic.shape[1] // 2
    block = 16

    def stack(step, carry):
        start = pl.multiple_of(step * block, block)
        totals = stack_sums(analytic, slots, start, block, lags, (0.0, 0.0, 0.0))
        for index, total in enumerate(totals):
            held[index, pl.ds(start, block)] = total
        return carry

    lax.fori_loop(0, lags // block, stack, 0, unroll=4)


def last_stacks(analytic, slots, held, weighted, forward_ref, spectrum, factor):
    lags, width = analytic.shape[1] // 2, analytic.shape[2] // NSRC
    half = width // 2
    block = 16

    def stack(step, carry):
        start = pl.multiple_of(step * block, block)
        totals = tuple(held[index, pl.ds(start, block)] for index in range(3))
        totals = stack_sums(analytic, slots, start, block, lags, totals)

        def fold(value):
            parts = []
            for s in range(NSRC):
                part = value[:, s * width : (s + 1) * width]
                parts.append(part + pltpu.roll(part, half, 1))
            side = lax.broadcasted_iota(jnp.int32, (block, width), 1) < half
            return jnp.where(side, parts[0], parts[1])

        linear, phase_re, phase_im = (fold(total) for total in totals)
        result = linear * (phase_re * phase_re + phase_im * phase_im) * factor
        weighted[pl.ds(start, block)] = result.astype(jnp.bfloat16)
        return carry

    lax.fori_loop(0, lags // block, stack, 0, unroll=4)
    result = lax.dot_general(
        weighted[...], forward_ref[...], (((0,), (0,)), ((), ())), preferred_element_type=jnp.float32
    )
    for part in range(lags // LANES):
        spectrum[part] = result[:, part * LANES : (part + 1) * LANES]


def phase_tables(offset_ref, base, phases, half, part):
    low = lax.broadcasted_iota(jnp.int32, (TILE, LANES), 0)
    freq = lax.broadcasted_iota(jnp.int32, (TILE, LANES), 1) + part * LANES
    product = low * freq

    def group(number, carry):
        for member in range(GROUP):
            channel = number * GROUP + member
            offset = offset_ref[base + channel]
            jump_cos, jump_sin = cos_sin(freq * (offset * TILE))
            cosine, sine = cos_sin(product * offset)
            phases[part, channel, 0] = cosine
            phases[part, channel, 1] = sine
            phases[part, channel, 2] = cosine * jump_cos + sine * jump_sin
            phases[part, channel, 3] = sine * jump_cos - cosine * jump_sin
            phases[part, channel, 4] = 2.0 * jump_cos
        return carry

    lax.fori_loop(0, half // GROUP, group, 0)


def slant(phases, spectrum, sums, half, bins, part, source):
    sums[part, source] = jnp.zeros(sums.shape[2:], jnp.float32)
    steps = NSLOW // TILE
    part_im = bins // LANES + part

    def group(number, carry):
        now, before, twice = [], [], []
        for member in range(SLANT_GROUP):
            channel = number * SLANT_GROUP + member
            cosine, sine = phases[part, channel, 0], phases[part, channel, 1]
            back_cos, back_sin = phases[part, channel, 2], phases[part, channel, 3]
            twice.append(phases[part, channel, 4])
            row = pl.ds(source * half + channel, 1)
            real, imag = spectrum[part, row], spectrum[part_im, row]
            now.append([real * cosine - imag * sine, real * sine + imag * cosine])
            before.append([real * back_cos - imag * back_sin, real * back_sin + imag * back_cos])
        for step in range(steps):
            for piece in range(2):
                total = now[0][piece]
                for member in range(1, SLANT_GROUP):
                    total = total + now[member][piece]
                here = (part, source, piece, pl.ds(step * TILE, TILE))
                sums[here] = sums[here] + total
            if step + 1 < steps:
                for member in range(SLANT_GROUP):
                    for piece in range(2):
                        later = twice[member] * now[member][piece] - before[member][piece]
                        before[member][piece] = now[member][piece]
                        now[member][piece] = later
        return carry

    lax.fori_loop(0, half // SLANT_GROUP, group, 0)


def kernel(
    windows, scaling, days, chans, spectra_hbm, sources_ref, offset_ref, inverse_hbm, forward_hbm, out_ref,
    kept, sent, got, column, columns_far, plane, columns_near, analytic, weighted, spectrum, sums, phases, held, spectra_ref,
    leaving, arriving, owned, landing, inverse_ref, forward_ref, table_sem,
    half_sem, far_sem, near_sem, leave_sem, own_sem,
):
    count, depth, width = spectra_ref.shape
    bins, half = depth // 2, width // 2
    parts = bins // LANES
    far = chans // NEAR
    rows = NSLOW // chans
    day, chan = lax.axis_index("days"), lax.axis_index("chan")
    high, low = chan // NEAR, chan % NEAR
    table_copies = [
        pltpu.make_async_copy(inverse_hbm, inverse_ref, table_sem.at[0]),
        pltpu.make_async_copy(forward_hbm, forward_ref, table_sem.at[1]),
    ]
    near_peers = [
        (dd, dl, (day + dd) % days, (low + dl) % NEAR)
        for dd in range(days)
        for dl in range(NEAR)
        if dd or dl
    ]
    far_peers = [
        (dd, dh, (day + dd) % days, (high + dh) % far)
        for dd in range(days)
        for dh in range(far)
        if dd or dh
    ]
    barrier = pltpu.get_barrier_semaphore()
    greeted = 0
    for dd, dl, to_day, to_low in near_peers:
        pl.semaphore_signal(
            barrier, inc=1, device_id={"days": to_day, "chan": high * NEAR + to_low},
            device_id_type=pl.DeviceIdType.MESH,
        )
        greeted += 1
    for dd, dh, to_day, to_high in far_peers:
        if dh:
            pl.semaphore_signal(
                barrier, inc=1, device_id={"days": to_day, "chan": to_high * NEAR + low},
                device_id_type=pl.DeviceIdType.MESH,
            )
            greeted += 1
    spectra_copy = pltpu.make_async_copy(spectra_hbm, spectra_ref, table_sem.at[2])
    spectra_copy.start()
    for copy in table_copies:
        copy.start()
    spectra_copy.wait()
    column[...] = source_columns(spectra_ref, sources_ref, chan)
    pack_halves(spectra_ref, kept, sent, day)
    pl.semaphore_wait(barrier, greeted)

    far_copies = []
    for dd, dh, to_day, to_high in far_peers:
        if dd == 0:
            copy = exchange(
                column, columns_far.at[dh - 1], far_sem.at[0, dh - 1], far_sem.at[1, dh - 1],
                day, to_high * NEAR + low,
            )
            copy.start()
            far_copies.append(copy)
    half_copy = exchange(sent, got, half_sem.at[0], half_sem.at[1], (day + 1) % days, chan)
    half_copy.start()
    phase_tables(offset_ref, day * half, phases, half, 0)
    total = column[...].astype(jnp.float32)
    for index, copy in enumerate(far_copies):
        copy.wait_recv()
        total = total + columns_far[index].astype(jnp.float32)
    plane[...] = total.astype(jnp.bfloat16)
    near_copies = []
    for index, (dd, dl, to_day, to_low) in enumerate(near_peers):
        copy = exchange(
            plane, columns_near.at[index], near_sem.at[0, index], near_sem.at[1, index],
            to_day, high * NEAR + to_low,
        )
        copy.start()
        near_copies.append((dd, copy))
    for part in range(1, parts):
        phase_tables(offset_ref, day * half, phases, half, part)

    def gather(wanted, value):
        for index, (dd, copy) in enumerate(near_copies):
            if dd == wanted:
                copy.wait_recv()
                value = value + columns_near[index].astype(jnp.float32)
        return value.astype(jnp.bfloat16)

    pairs = count // 2
    rows_own = gather(0, total)
    for copy in table_copies:
        copy.wait()
    correlate(kept, rows_own, inverse_ref, analytic, 0)
    first_stacks(analytic, range(pairs), held)
    rows_other = gather(1, 0.0)
    half_copy.wait_recv()
    correlate(got, rows_other, inverse_ref, analytic, pairs)
    others = range(pairs, 2 * pairs)
    last_stacks(analytic, others, held, weighted, forward_ref, spectrum, scaling / windows**3)

    leave_copies = []
    wire = leaving.dtype
    for turn in range(days):
        shift = days - 1 - turn
        target = (day + shift) % days
        for part in range(parts):
            slant(phases, spectrum, sums, half, bins, part, target)
            for lo in range(NEAR):
                for hi in range(far):
                    first = (hi * NEAR + lo) * rows
                    leaving[part, lo, target, :, hi * rows : (hi + 1) * rows] = sums[
                        part, target, :, first : first + rows
                    ].astype(wire)
            for index, (dd, dl, to_day, to_low) in enumerate(near_peers):
                if dd == shift:
                    copy = exchange(
                        leaving.at[part, to_low, target], arriving.at[part, index],
                        leave_sem.at[0, part, index], leave_sem.at[1, part, index],
                        target, high * NEAR + to_low,
                    )
                    copy.start()
                    leave_copies.append((part, index, copy))
    for part in range(parts):
        total = leaving[part, low, day].astype(jnp.float32)
        for at, index, copy in leave_copies:
            if at == part:
                copy.wait_recv()
                total = total + arriving[part, index].astype(jnp.float32)
        for hi in range(far):
            owned[hi, part] = total[:, hi * rows : (hi + 1) * rows].astype(wire)
    own_copies = []
    for index, (dd, dh, to_day, to_high) in enumerate(far_peers):
        copy = exchange(
            owned.at[to_high], landing.at[index], own_sem.at[0, index], own_sem.at[1, index],
            to_day, to_high * NEAR + low,
        )
        copy.start()
        own_copies.append((dd, index, copy))
    for shift in range(days):
        total = owned[high].astype(jnp.float32) if shift == 0 else 0.0
        for dd, index, copy in own_copies:
            if dd == shift:
                copy.wait_recv()
                total = total + landing[index].astype(jnp.float32)
        for part in range(parts):
            for piece in range(2):
                out_ref[:, (day + shift) % days, part, piece] = total[part, piece]
    half_copy.wait_send()
    for copy in far_copies:
        copy.wait_send()
    for dd, copy in near_copies:
        copy.wait_send()
    for part, index, copy in leave_copies:
        copy.wait_send()
    for dd, index, copy in own_copies:
        copy.wait_send()


def shards(spectra, sources, offsets):
    count, depth, width = spectra.shape
    bins, half = depth // 2, width // 2
    days, chans = lax.axis_size("days"), lax.axis_size("chan")
    windows = count * days
    inverse, forward = tables(bins)
    scaling = windows**1.5 / math.sqrt(width * chans)
    far, rows, parts, pairs = chans // NEAR, NSLOW // chans, bins // LANES, count // 2
    near_count, far_count = days * NEAR - 1, days * far - 1
    wire = jnp.bfloat16 if rows % TILE == 0 else jnp.float32
    vmem = pl.BlockSpec(memory_space=pltpu.VMEM)
    smem = pl.BlockSpec(memory_space=pltpu.SMEM)
    anywhere = pl.BlockSpec(memory_space=pl.ANY)
    bf16, f32 = jnp.bfloat16, jnp.float32
    dma = pltpu.SemaphoreType.DMA
    out = pl.pallas_call(
        functools.partial(kernel, windows, scaling, days, chans),
        out_shape=jax.ShapeDtypeStruct((rows, NSRC, parts, 2, LANES), f32),
        in_specs=[anywhere, smem, smem, anywhere, anywhere],
        out_specs=vmem,
        scratch_shapes=[
            pltpu.VMEM((pairs, depth, width), bf16),
            pltpu.VMEM((pairs, depth, width), bf16),
            pltpu.VMEM((pairs, depth, width), bf16),
            pltpu.VMEM((count * NSRC, depth), bf16),
            pltpu.VMEM((far - 1, count * NSRC, depth), bf16),
            pltpu.VMEM((count * NSRC, depth), bf16),
            pltpu.VMEM((near_count, count * NSRC, depth), bf16),
            pltpu.VMEM((2 * pairs, 2 * depth, NSRC * width), f32),
            pltpu.VMEM((depth, width), bf16),
            pltpu.VMEM((depth // LANES, NSRC * half, LANES), f32),
            pltpu.VMEM((parts, NSRC, 2, NSLOW, LANES), f32),
            pltpu.VMEM((parts, half, 5, TILE, LANES), f32),
            pltpu.VMEM((3, depth, NSRC * width), f32),
            pltpu.VMEM((count, depth, width), bf16),
            pltpu.VMEM((parts, NEAR, NSRC, 2, far * rows, LANES), wire),
            pltpu.VMEM((parts, near_count, 2, far * rows, LANES), wire),
            pltpu.VMEM((far, parts, 2, rows, LANES), wire),
            pltpu.VMEM((far_count, parts, 2, rows, LANES), wire),
            pltpu.VMEM(inverse.shape, bf16),
            pltpu.VMEM(forward.shape, bf16),
            dma((3,)),
            dma((2,)),
            dma((2, far - 1)),
            dma((2, near_count)),
            dma((2, parts, near_count)),
            dma((2, far_count)),
        ],
        compiler_params=pltpu.CompilerParams(collective_id=0, has_side_effects=True),
    )(spectra, sources, offsets, jnp.asarray(inverse), jnp.asarray(forward))
    return out.transpose(0, 1, 3, 2, 4).reshape(rows, NSRC, 2, bins)


def solution(mesh):
    placed = (P("days", None, "chan"), P(), P("chan"))
    return jax.shard_map(
        shards, mesh=mesh, in_specs=placed, out_specs=P("chan", None, None, None), check_vma=False
    )
```
